256 devices in a mesh: section: 4 (over x), row: 8 (over z), col: 8 (over y, core).
Axes of the slice: x: 4, y: 4, z: 8, core: 2. Of those that a mesh axis runs over, the one named last changes fastest.
Arguments:
- statistic: float32 [8192, 2048], P(('section', 'row'), 'col'), parts along dimension 0, as said below
- gradient: bfloat16 [8192, 28672], P('section', ('row', 'col')), parts along dimension 0, may hold values from -6 to 6
Outputs:
- next_m: float32 [8192, 2048], P(('section', 'row'), 'col'), parts along dimension 0
- preconditioned: bfloat16 [8192, 28672], P('section', ('row', 'col')), parts along dimension 0
- next_diag: float32 [8192], P(('section', 'row')), parts along dimension 0
The draws below stay inside these ranges and needn't reach their ends.
There are 4 independent parts, one for each index of `section`. The reference program is written for one: setup_inputs(seed, part) draws one part's arguments, and reference() takes and returns one part's arrays. A program takes and returns all parts, laid end to end along the dimension named above; each array names one. Nothing has to cross between parts.
Inputs may be any that keep to these rules, and one draw needn't show every extreme that they name: `statistic`: symmetric and positive definite.
All inputs are finite; a program needn't handle non-finite values.
Results may differ from the reference program's by a relative error of at most 0.0052.
Values may be sent and summed in bfloat16 or wider, within the bound.
No kernel may reach another device: no remote copies, remote signals or barrier semaphores. Data moves between devices by JAX's collectives and lax.ppermute only.
A program may use at most 64 MiB of HBM per device.

```python
import math
import jax
import jax.numpy as jnp
from jax import lax

BLOCK = 2048
FF = 28672


def draw_statistic(key, part):
    first, second = jax.random.split(jax.random.fold_in(key, 11), 2)
    places = jnp.arange(BLOCK, dtype=jnp.float32)
    ramp = 1.0 + 2.0 * places / BLOCK
    noise = jax.random.normal(first, (BLOCK, BLOCK), jnp.float32)
    scales = ramp * jnp.exp(jax.random.uniform(second, (BLOCK,), jnp.float32, 0.0, math.log(6.0)))
    symmetric = (noise + noise.T) * (0.70710678 / math.sqrt(BLOCK))
    inner = symmetric + 2.5 * jnp.eye(BLOCK, dtype=jnp.float32)
    roots = jnp.sqrt(scales)
    return roots[:, None] * inner * roots[None, :]


def level_of(rng, dims, pieces, least, top_value):
    level = 1.0
    for dim, parts in pieces:
        steps = jax.random.uniform(jax.random.fold_in(jax.random.fold_in(rng, 6), dim), (parts,), jnp.float32, least / len(pieces), top_value / len(pieces))
        level = level * jnp.repeat(jnp.exp(steps), dims[dim] // parts).reshape((-1,) + (1,) * (len(dims) - 1 - dim))
    return level


def normal_values(key, dims, spread, most, pieces=(), kind=jnp.bfloat16):
    gain = level_of(key, dims, pieces, -0.22, 0.18) if pieces else 1.0
    entries = jax.random.normal(key, dims, jnp.float32) * spread * gain
    return jnp.minimum(jnp.maximum(entries, -most), most).astype(kind)


def setup_inputs(seed: int = 0, part: int = 0) -> dict:
    arg_keys = jax.random.split(jax.random.key(seed), 3)
    part_splits = jax.random.split(jax.random.fold_in(arg_keys[2], part), 3)
    statistic = draw_statistic(jax.random.fold_in(jax.random.fold_in(arg_keys[2], part), 71), part)
    gradient = normal_values(part_splits[1], (BLOCK, FF), 1.0, 6.0, ((1, 64),))
    return dict(statistic=statistic, gradient=gradient)


def reference(statistic, gradient):
    highest = lax.Precision.HIGHEST
    total = jnp.sum(statistic * statistic)
    scale4 = jnp.sqrt(BLOCK * (total / (BLOCK * BLOCK) + 1e-06))
    m_start = statistic / scale4
    ident = jnp.eye(BLOCK, dtype=jnp.float32)
    t_mat = (5.0 * ident - m_start) / 4.0
    square = jnp.dot(t_mat, t_mat, precision=highest, preferred_element_type=jnp.float32)
    third = jnp.dot(square, m_start, precision=highest, preferred_element_type=jnp.float32)
    full = jnp.dot(square, third, precision=highest, preferred_element_type=jnp.float32)
    next_m = full * (1.0 - ident)
    next_diag = jnp.diagonal(full)
    x_next = (t_mat / jnp.sqrt(jnp.sqrt(scale4))).astype(jnp.bfloat16)
    preconditioned = jnp.dot(x_next, gradient, preferred_element_type=jnp.float32).astype(jnp.bfloat16)
    return (next_m, preconditioned, next_diag)
```

```python
import jax
import jax.numpy as jnp
from jax import lax
from jax.experimental import pallas as pl
from jax.experimental.pallas import tpu as pltpu
from jax.sharding import PartitionSpec as P

BLOCK = 2048
SIDE = 256
HALF = 128
ROWS = 144
GRID = 8
F32 = jnp.float32
BF16 = jnp.bfloat16


def eye_mask(n):
    a = lax.broadcasted_iota(jnp.int32, (n, n), 0)
    b = lax.broadcasted_iota(jnp.int32, (n, n), 1)
    return a, b


def three_parts(x):
    hi = x.astype(BF16)
    rest = x - hi.astype(F32)
    mid = rest.astype(BF16)
    low = (rest - mid.astype(F32)).astype(BF16)
    return [hi.astype(F32), mid.astype(F32), low.astype(F32)]


def prep_body(where_ref, s_ref, out_ref):
    row, col = where_ref[0], where_ref[1]
    copies = out_ref.shape[0]
    s = s_ref[...]
    a, b = eye_mask(SIDE)
    squares = jnp.sum(s * s, axis=0, keepdims=True)
    diag = jnp.sum(jnp.where((a == b) & (row == col), s, 0.0), axis=0, keepdims=True)
    tail = three_parts(diag) + three_parts(squares) + [jnp.zeros((ROWS - HALF - 6, SIDE), F32)]
    tail = jnp.concatenate(tail, axis=0).astype(BF16)

    def put(half):
        half = half.astype(BF16)
        for n in range(copies):
            out_ref[n, :HALF, :] = half
            out_ref[n, HALF:, :] = tail

    @pl.when(row < col)
    def _():
        put(s[:HALF, :])

    @pl.when(row > col)
    def _():
        put(s[:, HALF:].T)

    @pl.when(row == col)
    def _():
        p, q = eye_mask(HALF)
        upper = jnp.where(p < q, s[:HALF, :HALF], 0.0)
        lower = jnp.where(p > q, s[HALF:, HALF:], 0.0)
        put(jnp.concatenate([upper + lower, s[:HALF, HALF:]], axis=1))


def prep(where, statistic, copies):
    return pl.pallas_call(
        prep_body,
        out_shape=jax.ShapeDtypeStruct((copies, ROWS, SIDE), BF16),
        in_specs=[
            pl.BlockSpec(memory_space=pltpu.SMEM),
            pl.BlockSpec(memory_space=pltpu.VMEM),
        ],
        out_specs=pl.BlockSpec(memory_space=pltpu.VMEM),
    )(where, statistic)


def block_of(size, index):
    return pl.ds(pl.multiple_of(index * size, size), size)


def main_body(where_ref, own_ref, other_ref, g_ref, m_ref, pre_ref, nd_ref, o_ref, dcol_ref,
              v_ref, t_ref, th_ref, third_ref, oa_ref, ob_ref):
    row, col, core = where_ref[0], where_ref[1], where_ref[2]
    a, b = eye_mask(SIDE)
    same = a == b
    p, q = eye_mask(HALF)
    twin = [own_ref, other_ref]

    def piece(i, j, rows):
        src = twin[j % 2]
        return src[j // 2, i, rows, :]

    squares = jnp.zeros((1, SIDE), F32)
    drows = []
    for i in range(GRID):
        for j in range(GRID):
            tail = piece(i, j, slice(HALF, ROWS)).astype(F32)
            squares = squares + (tail[3:4] + tail[4:5] + tail[5:6])
            if i == j:
                drow = tail[0:1] + tail[1:2] + tail[2:3]
                drows.append(drow)
                dcol_ref[i * SIDE : (i + 1) * SIDE, :] = jnp.sum(
                    jnp.where(same, drow, 0.0), axis=1, keepdims=True
                )
    total = jnp.sum(squares)
    ss = jnp.full((1, 1), total, F32)
    scale = jnp.sqrt(BLOCK * (ss / (BLOCK * BLOCK) + 1e-06))
    inv = 1.0 / scale
    for i in range(GRID):
        here = slice(i * SIDE, (i + 1) * SIDE)
        both = piece(i, i, slice(0, HALF))
        mixed = both[:, :HALF].astype(F32)
        corner = both[:, HALF:]
        upper = jnp.where(p < q, mixed, 0.0)
        lower = jnp.where(p > q, mixed, 0.0)
        o_ref[i * SIDE : i * SIDE + HALF, i * SIDE : i * SIDE + HALF] = (upper + upper.T).astype(BF16)
        o_ref[i * SIDE + HALF : (i + 1) * SIDE, i * SIDE + HALF : (i + 1) * SIDE] = (
            lower + lower.T
        ).astype(BF16)
        o_ref[i * SIDE : i * SIDE + HALF, i * SIDE + HALF : (i + 1) * SIDE] = corner
        o_ref[i * SIDE + HALF : (i + 1) * SIDE, i * SIDE : i * SIDE + HALF] = corner.T
        for j in range(i + 1, GRID):
            there = slice(j * SIDE, (j + 1) * SIDE)
            block = jnp.concatenate(
                [piece(i, j, slice(0, HALF)), piece(j, i, slice(0, HALF))], axis=0
            )
            o_ref[here, there] = block
            o_ref[there, here] = block.T

    v_ref[:, :SIDE] = o_ref[:, block_of(SIDE, row)]
    v_ref[:, SIDE:] = o_ref[:, block_of(SIDE, col)]

    def row_of(index):
        return jnp.sum(jnp.where(same, dcol_ref[block_of(SIDE, index), :], 0.0), axis=0, keepdims=True)

    d_cols = jnp.concatenate([row_of(row), row_of(col)], axis=1)
    lanes = lax.broadcasted_iota(jnp.int32, (SIDE, 2 * SIDE), 1)
    col_ids = jnp.where(lanes < SIDE, row * SIDE + lanes, (col - 1) * SIDE + lanes)
    sub = lax.broadcasted_iota(jnp.int32, (SIDE, 2 * SIDE), 0)

    def two(n, _):
        rows = block_of(SIDE, n)
        w = jnp.dot(o_ref[rows, :], v_ref[...], preferred_element_type=F32)
        o = v_ref[rows, :].astype(F32)
        d = dcol_ref[rows, :]
        on = (sub + n * SIDE) == col_ids
        sq = jnp.where(on, d * d, 0.0) + (d + d_cols) * o + w
        mine = jnp.where(on, d, 0.0) + o
        t = (jnp.where(on, 25.0, 0.0) - (10.0 * inv) * mine + (inv * inv) * sq) * 0.0625
        t_ref[rows, :] = t
        th_ref[rows, :] = jnp.where(on, 0.0, t).astype(BF16)
        return 0

    lax.fori_loop(0, GRID, two, 0)

    own_t = jnp.concatenate([t_ref[block_of(SIDE, row), :SIDE], t_ref[block_of(SIDE, col), SIDE:]], axis=1)
    e_cols = jnp.sum(
        jnp.where(jnp.concatenate([same, same], axis=1), own_t, 0.0), axis=0, keepdims=True
    )

    def three(n, acc):
        rows = block_of(SIDE, n)
        w = jnp.dot(o_ref[rows, :], th_ref[...], preferred_element_type=F32)
        o = v_ref[rows, :].astype(F32)
        t = t_ref[rows, :]
        third = (dcol_ref[rows, :] * t + o * e_cols + w) * inv
        third_ref[rows, :] = third[:, SIDE:]
        on = (sub + n * SIDE) == col_ids
        ob_ref[rows, :] = jnp.where(on, 0.0, third)[:, SIDE:].astype(BF16)
        return acc + jnp.sum(t[:, :SIDE] * third[:, :SIDE], axis=0, keepdims=True)

    nd_ref[...] = lax.fori_loop(0, GRID, three, jnp.zeros((1, SIDE), F32))

    inner = lax.dot_general(
        th_ref[:, :SIDE], ob_ref[...], (((0,), (0,)), ((), ())), preferred_element_type=F32
    )
    e_row = jnp.sum(jnp.where(same, t_ref[block_of(SIDE, row), :SIDE], 0.0), axis=1, keepdims=True)
    third_col = jnp.sum(
        jnp.where(same, third_ref[block_of(SIDE, col), :], 0.0), axis=0, keepdims=True
    )
    full = e_row * third_ref[block_of(SIDE, row), :] + t_ref[block_of(SIDE, row), SIDE:] * third_col + inner
    m_ref[...] = jnp.where(same & (row == col), 0.0, full)

    root = lax.rsqrt(jnp.sqrt(scale))

    def spread(n, _):
        rows = block_of(SIDE, n)
        w = jnp.dot(o_ref[rows, :], g_ref[...], preferred_element_type=F32)
        g = g_ref[rows, :].astype(F32)
        w = w + dcol_ref[rows, :] * g
        pre_ref[rows, :] = ((1.25 * g - (0.25 * inv) * w) * root).astype(BF16)
        return 0

    lax.fori_loop(0, GRID, spread, 0)


def main(where, own, other, gradient):
    wide = gradient.shape[1]
    vmem = pl.BlockSpec(memory_space=pltpu.VMEM)
    return pl.pallas_call(
        main_body,
        out_shape=(
            jax.ShapeDtypeStruct((SIDE, SIDE), F32),
            jax.ShapeDtypeStruct((BLOCK, wide), BF16),
            jax.ShapeDtypeStruct((1, SIDE), F32),
        ),
        in_specs=[pl.BlockSpec(memory_space=pltpu.SMEM), vmem, vmem, vmem],
        out_specs=(vmem, vmem, vmem),
        scratch_shapes=[
            pltpu.VMEM((BLOCK, BLOCK), BF16),
            pltpu.VMEM((BLOCK, 1), F32),
            pltpu.VMEM((BLOCK, 2 * SIDE), BF16),
            pltpu.VMEM((BLOCK, 2 * SIDE), F32),
            pltpu.VMEM((BLOCK, 2 * SIDE), BF16),
            pltpu.VMEM((BLOCK, SIDE), F32),
            pltpu.VMEM((8, 128), BF16),
            pltpu.VMEM((BLOCK, SIDE), BF16),
        ],
        compiler_params=pltpu.CompilerParams(vmem_limit_bytes=56 * 1024 * 1024),
    )(where, own, other, gradient)


SAME_CORE = [[0, 2, 4, 6], [1, 3, 5, 7]]


def local(statistic, gradient):
    row, col = lax.axis_index("row"), lax.axis_index("col")
    core = lax.rem(col, 2)
    where = jnp.stack([row, col, core]).astype(jnp.int32)
    mine = prep(where, statistic, GRID)
    along = lax.all_to_all(mine, "row", split_axis=0, concat_axis=0, tiled=True)
    sent = jnp.broadcast_to(along, (4, *along.shape))
    own = lax.all_to_all(
        sent, "col", split_axis=0, concat_axis=0, tiled=True, axis_index_groups=SAME_CORE
    )
    twin = lax.ppermute(own, "col", [(i, i ^ 1) for i in range(8)])
    even = jnp.where(core == 0, own, twin)
    odd = jnp.where(core == 0, twin, own)
    next_m, preconditioned, next_diag = main(where, even, odd, gradient)
    return (next_m, preconditioned, next_diag.reshape(SIDE))


def solution(mesh):
    return jax.shard_map(
        local,
        mesh=mesh,
        in_specs=(P(("section", "row"), "col"), P("section", ("row", "col"))),
        out_specs=(
            P(("section", "row"), "col"),
            P("section", ("row", "col")),
            P(("section", "row")),
        ),
        check_vma=False,
    )
```

```python
import jax
import jax.numpy as jnp
from jax import lax
from jax.experimental import pallas as pl
from jax.experimental.pallas import tpu as pltpu
from jax.sharding import PartitionSpec as P

BLOCK = 2048
SIDE = 256
HALF = 128
ROWS = 144
GRID = 8
F32 = jnp.float32
BF16 = jnp.bfloat16


def eye_mask(n):
    a = lax.broadcasted_iota(jnp.int32, (n, n), 0)
    b = lax.broadcasted_iota(jnp.int32, (n, n), 1)
    return a, b


def three_parts(x):
    hi = x.astype(BF16)
    rest = x - hi.astype(F32)
    mid = rest.astype(BF16)
    low = (rest - mid.astype(F32)).astype(BF16)
    return [hi.astype(F32), mid.astype(F32), low.astype(F32)]


def prep_body(where_ref, s_ref, out_ref):
    row, col = where_ref[0], where_ref[1]
    s = s_ref[...]
    a, b = eye_mask(SIDE)
    squares = jnp.sum(s * s, axis=0, keepdims=True)
    diag = jnp.sum(jnp.where((a == b) & (row == col), s, 0.0), axis=0, keepdims=True)
    tail = three_parts(diag) + three_parts(squares) + [jnp.zeros((ROWS - HALF - 6, SIDE), F32)]
    out_ref[HALF:, :] = jnp.concatenate(tail, axis=0).astype(BF16)

    @pl.when(row < col)
    def _():
        out_ref[:HALF, :] = s[:HALF, :].astype(BF16)

    @pl.when(row > col)
    def _():
        out_ref[:HALF, :] = s[:, HALF:].T.astype(BF16)

    @pl.when(row == col)
    def _():
        p, q = eye_mask(HALF)
        upper = jnp.where(p < q, s[:HALF, :HALF], 0.0)
        lower = jnp.where(p > q, s[HALF:, HALF:], 0.0)
        out_ref[:HALF, :HALF] = (upper + lower).astype(BF16)
        out_ref[:HALF, HALF:] = s[:HALF, HALF:].astype(BF16)


def prep(where, statistic):
    return pl.pallas_call(
        prep_body,
        out_shape=jax.ShapeDtypeStruct((ROWS, SIDE), BF16),
        in_specs=[
            pl.BlockSpec(memory_space=pltpu.SMEM),
            pl.BlockSpec(memory_space=pltpu.VMEM),
        ],
        out_specs=pl.BlockSpec(memory_space=pltpu.VMEM),
    )(where, statistic)


def block_of(size, index):
    return pl.ds(pl.multiple_of(index * size, size), size)


TILE = 512


def main_body(where_ref, own_ref, twin_ref, g_hbm, m_ref, pre_hbm, nd_ref, h_ref, g_ref, pre_ref,
              o_ref, dcol_ref, drow_ref, v_ref, t_ref, th_ref, third_ref, ob_ref, in_sem, out_sem):
    row, col, core = where_ref[0], where_ref[1], where_ref[2]
    a, b = eye_mask(SIDE)
    same = a == b
    p, q = eye_mask(HALF)
    arrivals = [
        pltpu.make_async_copy(own_ref, h_ref.at[core], in_sem.at[0]),
        pltpu.make_async_copy(twin_ref, h_ref.at[1 - core], in_sem.at[1]),
        pltpu.make_async_copy(g_hbm, g_ref, in_sem.at[2]),
    ]
    for copy in arrivals:
        copy.start()

    def ring_slot(offset, size):
        middle = size // 2
        return jnp.where(
            offset < middle, 2 * offset, jnp.where(offset == middle, size - 1, 2 * (size - offset) - 1)
        )

    row_slot = [ring_slot(lax.rem(i - row + GRID, GRID), GRID) for i in range(GRID)]
    pair = col // 2
    pair_slot = [ring_slot(lax.rem(j - pair + 4, 4), 4) for j in range(4)]

    def piece(i, j, rows):
        return h_ref[j % 2, pair_slot[j // 2] * GRID + row_slot[i], rows, :]

    arrivals[0].wait()
    arrivals[1].wait()

    squares = jnp.zeros((1, SIDE), F32)
    for i in range(GRID):
        here = slice(i * SIDE, (i + 1) * SIDE)
        for j in range(GRID):
            tail = piece(i, j, slice(HALF, ROWS)).astype(F32)
            squares = squares + (tail[3:4] + tail[4:5] + tail[5:6])
            if i == j:
                drow = tail[0:1] + tail[1:2] + tail[2:3]
                drow_ref[:, here] = drow
                dcol_ref[here, :] = jnp.sum(jnp.where(same, drow, 0.0), axis=1, keepdims=True)
    ss = jnp.full((1, 1), jnp.sum(squares), F32)
    scale = jnp.sqrt(BLOCK * (ss / (BLOCK * BLOCK) + 1e-06))
    inv = 1.0 / scale
    root = lax.rsqrt(jnp.sqrt(scale))
    for i in range(GRID):
        here = slice(i * SIDE, (i + 1) * SIDE)
        first = slice(i * SIDE, i * SIDE + HALF)
        second = slice(i * SIDE + HALF, (i + 1) * SIDE)
        both = piece(i, i, slice(0, HALF))
        mixed = both[:, :HALF].astype(F32)
        corner = both[:, HALF:]
        upper = jnp.where(p < q, mixed, 0.0)
        lower = jnp.where(p > q, mixed, 0.0)
        o_ref[first, first] = (upper + upper.T).astype(BF16)
        o_ref[second, second] = (lower + lower.T).astype(BF16)
        o_ref[first, second] = corner
        o_ref[second, first] = corner.T
        for j in range(i + 1, GRID):
            there = slice(j * SIDE, (j + 1) * SIDE)
            block = jnp.concatenate(
                [piece(i, j, slice(0, HALF)), piece(j, i, slice(0, HALF))], axis=0
            )
            o_ref[here, there] = block
            o_ref[there, here] = block.T

    arrivals[2].wait()

    def leave(n):
        cols = block_of(TILE, n)
        return pltpu.make_async_copy(pre_ref.at[:, cols], pre_hbm.at[:, cols], out_sem.at[n])

    def spread(n, _):
        cols = block_of(TILE, n)
        w = jnp.dot(g_ref[...], o_ref[:, cols], preferred_element_type=F32)
        g = g_ref[:, cols].astype(F32)
        near = (1.25 * root) - (0.25 * inv * root) * drow_ref[:, cols]
        pre_ref[:, cols] = (near * g - (0.25 * inv * root) * w).astype(BF16)
        leave(n).start()
        return 0

    lax.fori_loop(0, BLOCK // TILE, spread, 0)

    v_ref[:, :SIDE] = o_ref[:, block_of(SIDE, row)]
    v_ref[:, SIDE:] = o_ref[:, block_of(SIDE, col)]
    d_cols = jnp.concatenate([drow_ref[:, block_of(SIDE, row)], drow_ref[:, block_of(SIDE, col)]], axis=1)
    lanes = lax.broadcasted_iota(jnp.int32, (TILE, 2 * SIDE), 1)
    col_ids = jnp.where(lanes < SIDE, row * SIDE + lanes, (col - 1) * SIDE + lanes)
    sub = lax.broadcasted_iota(jnp.int32, (TILE, 2 * SIDE), 0)

    def two(n, _):
        rows = block_of(TILE, n)
        w = jnp.dot(o_ref[rows, :], v_ref[...], preferred_element_type=F32)
        o = v_ref[rows, :].astype(F32)
        d = dcol_ref[rows, :]
        on = (sub + n * TILE) == col_ids
        sq = jnp.where(on, d * d, 0.0) + (d + d_cols) * o + w
        mine = jnp.where(on, d, 0.0) + o
        t = (jnp.where(on, 25.0, 0.0) - (10.0 * inv) * mine + (inv * inv) * sq) * 0.0625
        t_ref[rows, :] = t
        th_ref[rows, :] = jnp.where(on, 0.0, t).astype(BF16)
        return 0

    lax.fori_loop(0, BLOCK // TILE, two, 0)

    own_t = jnp.concatenate([t_ref[block_of(SIDE, row), :SIDE], t_ref[block_of(SIDE, col), SIDE:]], axis=1)
    e_cols = jnp.sum(
        jnp.where(jnp.concatenate([same, same], axis=1), own_t, 0.0), axis=0, keepdims=True
    )

    def three(n, acc):
        rows = block_of(TILE, n)
        w = jnp.dot(o_ref[rows, :], th_ref[...], preferred_element_type=F32)
        o = v_ref[rows, :].astype(F32)
        t = t_ref[rows, :]
        third = (dcol_ref[rows, :] * t + o * e_cols + w) * inv
        third_ref[rows, :] = third[:, SIDE:]
        on = (sub + n * TILE) == col_ids
        ob_ref[rows, :] = jnp.where(on, 0.0, third)[:, SIDE:].astype(BF16)
        return acc + jnp.sum(t[:, :SIDE] * third[:, :SIDE], axis=0, keepdims=True)

    nd_ref[...] = lax.fori_loop(0, BLOCK // TILE, three, jnp.zeros((1, SIDE), F32))

    inner = lax.dot_general(
        th_ref[:, :SIDE], ob_ref[...], (((0,), (0,)), ((), ())), preferred_element_type=F32
    )
    e_row = jnp.sum(jnp.where(same, t_ref[block_of(SIDE, row), :SIDE], 0.0), axis=1, keepdims=True)
    third_col = jnp.sum(
        jnp.where(same, third_ref[block_of(SIDE, col), :], 0.0), axis=0, keepdims=True
    )
    full = e_row * third_ref[block_of(SIDE, row), :] + t_ref[block_of(SIDE, row), SIDE:] * third_col + inner
    m_ref[...] = jnp.where(same & (row == col), 0.0, full)
    for n in range(BLOCK // TILE):
        leave(n).wait()


def main(where, own, twin, gradient):
    wide = gradient.shape[0]
    vmem = pl.BlockSpec(memory_space=pltpu.VMEM)
    hbm = pl.BlockSpec(memory_space=pl.ANY)
    return pl.pallas_call(
        main_body,
        out_shape=(
            jax.ShapeDtypeStruct((SIDE, SIDE), F32),
            jax.ShapeDtypeStruct((wide, BLOCK), BF16),
            jax.ShapeDtypeStruct((1, SIDE), F32),
        ),
        in_specs=[pl.BlockSpec(memory_space=pltpu.SMEM), hbm, hbm, hbm],
        out_specs=(vmem, hbm, vmem),
        scratch_shapes=[
            pltpu.VMEM((2, *own.shape), BF16),
            pltpu.VMEM((wide, BLOCK), BF16),
            pltpu.VMEM((wide, BLOCK), BF16),
            pltpu.VMEM((BLOCK, BLOCK), BF16),
            pltpu.VMEM((BLOCK, 1), F32),
            pltpu.VMEM((1, BLOCK), F32),
            pltpu.VMEM((BLOCK, 2 * SIDE), BF16),
            pltpu.VMEM((BLOCK, 2 * SIDE), F32),
            pltpu.VMEM((BLOCK, 2 * SIDE), BF16),
            pltpu.VMEM((BLOCK, SIDE), F32),
            pltpu.VMEM((BLOCK, SIDE), BF16),
            pltpu.SemaphoreType.DMA((3,)),
            pltpu.SemaphoreType.DMA((BLOCK // TILE,)),
        ],
        compiler_params=pltpu.CompilerParams(vmem_limit_bytes=56 * 1024 * 1024),
    )(where, own, twin, gradient)


def shifted(x, axis, step):
    size = lax.axis_size(axis)
    return lax.ppermute(x, axis, [(i, (i + step) % size) for i in range(size)])


def gathered(half):
    up, down = shifted(half, "row", 1), shifted(half, "row", -1)
    up2, down2 = shifted(half, "row", 2), shifted(half, "row", -2)
    up3, down3 = shifted(up, "row", 2), shifted(down, "row", -2)
    up4 = shifted(up2, "row", 2)
    line = jnp.stack([half, up, down, up2, down2, up3, down3, up4])
    over, under = shifted(line, "col", 2), shifted(line, "col", -2)
    far = [shifted(over[:4], "col", 2), shifted(under[4:], "col", -2)]
    return jnp.concatenate([line, over, under, *far])


def local(statistic, gradient):
    row, col = lax.axis_index("row"), lax.axis_index("col")
    where = jnp.stack([row, col, lax.rem(col, 2)]).astype(jnp.int32)
    own = gathered(prep(where, statistic))
    twin = lax.ppermute(own, "col", [(i, i ^ 1) for i in range(GRID)])
    next_m, preconditioned, next_diag = main(where, own, twin, gradient.T)
    return (next_m, preconditioned.T, next_diag.reshape(SIDE))


def solution(mesh):
    return jax.shard_map(
        local,
        mesh=mesh,
        in_specs=(P(("section", "row"), "col"), P("section", ("row", "col"))),
        out_specs=(
            P(("section", "row"), "col"),
            P("section", ("row", "col")),
            P(("section", "row")),
        ),
        check_vma=False,
    )
```

```python
import jax
import jax.numpy as jnp
from jax import lax
from jax.experimental import pallas as pl
from jax.experimental.pallas import tpu as pltpu
from jax.sharding import PartitionSpec as P

BLOCK = 2048
SIDE = 256
HALF = 128
ROWS = 144
GRID = 8
F32 = jnp.float32
BF16 = jnp.bfloat16


def eye_mask(n):
    a = lax.broadcasted_iota(jnp.int32, (n, n), 0)
    b = lax.broadcasted_iota(jnp.int32, (n, n), 1)
    return a, b


def three_parts(x):
    hi = x.astype(BF16)
    rest = x - hi.astype(F32)
    mid = rest.astype(BF16)
    low = (rest - mid.astype(F32)).astype(BF16)
    return [hi.astype(F32), mid.astype(F32), low.astype(F32)]


def prep_body(s_ref, out_ref):
    row, col = lax.axis_index("row"), lax.axis_index("col")
    s = s_ref[...]
    a, b = eye_mask(SIDE)
    squares = jnp.sum(s * s, axis=0, keepdims=True)
    diag = jnp.sum(jnp.where((a == b) & (row == col), s, 0.0), axis=0, keepdims=True)
    tail = three_parts(diag) + three_parts(squares) + [jnp.zeros((ROWS - HALF - 6, SIDE), F32)]
    out_ref[HALF:, :] = jnp.concatenate(tail, axis=0).astype(BF16)

    @pl.when(row < col)
    def _():
        out_ref[:HALF, :] = s[:HALF, :].astype(BF16)

    @pl.when(row > col)
    def _():
        out_ref[:HALF, :] = s[:, HALF:].T.astype(BF16)

    @pl.when(row == col)
    def _():
        p, q = eye_mask(HALF)
        upper = jnp.where(p < q, s[:HALF, :HALF], 0.0)
        lower = jnp.where(p > q, s[HALF:, HALF:], 0.0)
        out_ref[:HALF, :HALF] = (upper + lower).astype(BF16)
        out_ref[:HALF, HALF:] = s[:HALF, HALF:].astype(BF16)


def prep(statistic):
    return pl.pallas_call(
        prep_body,
        out_shape=jax.ShapeDtypeStruct((ROWS, SIDE), BF16),
        in_specs=[pl.BlockSpec(memory_space=pltpu.VMEM)],
        out_specs=pl.BlockSpec(memory_space=pltpu.VMEM),
    )(statistic)


def block_of(size, index):
    return pl.ds(pl.multiple_of(index * size, size), size)


TILE = 512


def main_body(own_ref, twin_ref, g_hbm, m_ref, pre_hbm, nd_ref, g_ref, pre_ref,
              o_ref, dcol_ref, drow_ref, v_ref, t_ref, th_ref, third_ref, ob_ref,
              in_sem, out_sem):
    row, col = lax.axis_index("row"), lax.axis_index("col")
    core = lax.rem(col, 2)
    a, b = eye_mask(SIDE)
    same = a == b
    p, q = eye_mask(HALF)
    arrival = pltpu.make_async_copy(g_hbm, g_ref, in_sem.at[0])
    arrival.start()

    def ring_slot(offset, size):
        middle = size // 2
        return jnp.where(
            offset < middle, 2 * offset, jnp.where(offset == middle, size - 1, 2 * (size - offset) - 1)
        )

    row_slot = [ring_slot(lax.rem(i - row + GRID, GRID), GRID) for i in range(GRID)]
    pair = col // 2
    pair_slot = [ring_slot(lax.rem(j - pair + 4, 4), 4) for j in range(4)]

    def slot_of(j, line):
        over, under, far = pair_slot[j] == 1, pair_slot[j] == 2, pair_slot[j] == 3
        first = jnp.where(over, 8, jnp.where(under, 13, jnp.where(far, 24, 0)))
        then = jnp.where(over, 13, jnp.where(under, 16, jnp.where(far, 24, 0)))
        return line + jnp.where(line < 5, first, then)

    def above(half, i, there):
        o_ref[i * SIDE : i * SIDE + HALF, there] = half
        o_ref[there, i * SIDE : i * SIDE + HALF] = half.T

    def below(half, second, i):
        o_ref[second, i * SIDE : (i + 1) * SIDE] = half
        o_ref[i * SIDE : (i + 1) * SIDE, second] = half.T

    def middle(half, i):
        first = slice(i * SIDE, i * SIDE + HALF)
        second = slice(i * SIDE + HALF, (i + 1) * SIDE)
        mixed = half[:, :HALF].astype(F32)
        corner = half[:, HALF:]
        upper = jnp.where(p < q, mixed, 0.0)
        lower = jnp.where(p > q, mixed, 0.0)
        o_ref[first, first] = (upper + upper.T).astype(BF16)
        o_ref[second, second] = (lower + lower.T).astype(BF16)
        o_ref[first, second] = corner
        o_ref[second, first] = corner.T

    def assemble(pieces_ref, parity):
        total = jnp.zeros((1, SIDE), F32)
        for j in range(4):
            there = block_of(SIDE, 2 * j + parity)
            second = pl.ds(pl.multiple_of((2 * j + parity) * SIDE + HALF, HALF), HALF)
            for i in range(GRID):
                slot = slot_of(j, row_slot[i])
                tail = pieces_ref[slot, HALF:ROWS, :].astype(F32)
                total = total + (tail[3:4] + tail[4:5] + tail[5:6])
                if i == 2 * j:

                    @pl.when(parity == 0)
                    def _():
                        middle(pieces_ref[slot, :HALF, :], i)

                    @pl.when(parity == 1)
                    def _():
                        above(pieces_ref[slot, :HALF, :], i, there)

                elif i == 2 * j + 1:

                    @pl.when(parity == 1)
                    def _():
                        middle(pieces_ref[slot, :HALF, :], i)

                    @pl.when(parity == 0)
                    def _():
                        below(pieces_ref[slot, :HALF, :], second, i)

                elif i < 2 * j:
                    above(pieces_ref[slot, :HALF, :], i, there)
                else:
                    below(pieces_ref[slot, :HALF, :], second, i)
            slot = slot_of(j, jnp.where(parity == 0, row_slot[2 * j], row_slot[2 * j + 1]))
            tail = pieces_ref[slot, HALF:ROWS, :].astype(F32)
            drow = tail[0:1] + tail[1:2] + tail[2:3]
            drow_ref[:, there] = drow
            dcol_ref[there, :] = jnp.sum(jnp.where(same, drow, 0.0), axis=1, keepdims=True)
        return total

    squares = assemble(own_ref, core) + assemble(twin_ref, 1 - core)
    ss = jnp.full((1, 1), jnp.sum(squares), F32)
    scale = jnp.sqrt(BLOCK * (ss / (BLOCK * BLOCK) + 1e-06))
    inv = 1.0 / scale
    root = lax.rsqrt(jnp.sqrt(scale))

    arrival.wait()

    def leave(n):
        cols = block_of(TILE, n)
        return pltpu.make_async_copy(pre_ref.at[:, cols], pre_hbm.at[:, cols], out_sem.at[n])

    far_by = 0.25 * inv * root

    def spread(n, _):
        cols = block_of(TILE, n)
        w = jnp.dot(g_ref[...], o_ref[:, cols], preferred_element_type=F32)
        near_by = (1.25 * root) - far_by * drow_ref[:, cols]
        pre_ref[:, cols] = (near_by * g_ref[:, cols].astype(F32) - far_by * w).astype(BF16)
        leave(n).start()
        return 0

    lax.fori_loop(0, BLOCK // TILE, spread, 0)

    v_ref[:, :SIDE] = o_ref[:, block_of(SIDE, row)]
    v_ref[:, SIDE:] = o_ref[:, block_of(SIDE, col)]
    d_cols = jnp.concatenate([drow_ref[:, block_of(SIDE, row)], drow_ref[:, block_of(SIDE, col)]], axis=1)
    second_by = 0.0625 * inv * inv
    by_col = second_by * d_cols - 0.625 * inv

    def two(n, _):
        rows = block_of(TILE, n)
        w = jnp.dot(o_ref[rows, :], v_ref[...], preferred_element_type=F32)
        t = (second_by * dcol_ref[rows, :] + by_col) * v_ref[rows, :].astype(F32) + second_by * w
        t_ref[rows, :] = t
        th_ref[rows, :] = t.astype(BF16)
        return 0

    lax.fori_loop(0, BLOCK // TILE, two, 0)

    ones = d_cols * inv
    alone = (25.0 - 10.0 * ones + ones * ones) * 0.0625
    diags = []
    for place, lanes in ((row, slice(0, SIDE)), (col, slice(SIDE, 2 * SIDE))):
        rows = block_of(SIDE, place)
        t = t_ref[rows, lanes] + jnp.where(same, alone[:, lanes], 0.0)
        t_ref[rows, lanes] = t
        th_ref[rows, lanes] = jnp.where(same, 0.0, t).astype(BF16)
        diags.append(jnp.where(same, t, 0.0))
    e_cols = jnp.concatenate([jnp.sum(x, axis=0, keepdims=True) for x in diags], axis=1)
    e_row = jnp.sum(diags[0], axis=1, keepdims=True)
    e_by = e_cols * inv

    def three(n, acc):
        rows = block_of(TILE, n)
        w = jnp.dot(o_ref[rows, :], th_ref[...], preferred_element_type=F32)
        t = t_ref[rows, :]
        third = (dcol_ref[rows, :] * inv) * t + v_ref[rows, :].astype(F32) * e_by + w * inv
        third_ref[rows, :] = third[:, SIDE:]
        ob_ref[rows, :] = third[:, SIDE:].astype(BF16)
        return acc + jnp.sum(t[:, :SIDE] * third[:, :SIDE], axis=0, keepdims=True)

    nd_ref[...] = lax.fori_loop(0, BLOCK // TILE, three, jnp.zeros((1, SIDE), F32))

    rows = block_of(SIDE, col)
    third = third_ref[rows, :]
    ob_ref[rows, :] = jnp.where(same, 0.0, third).astype(BF16)
    third_col = jnp.sum(jnp.where(same, third, 0.0), axis=0, keepdims=True)
    inner = lax.dot_general(
        th_ref[:, :SIDE], ob_ref[...], (((0,), (0,)), ((), ())), preferred_element_type=F32
    )
    rows = block_of(SIDE, row)
    full = e_row * third_ref[rows, :] + t_ref[rows, SIDE:] * third_col + inner
    m_ref[...] = jnp.where(same & (row == col), 0.0, full)
    for n in range(BLOCK // TILE):
        leave(n).wait()


def main(own, twin, gradient):
    wide = gradient.shape[0]
    vmem = pl.BlockSpec(memory_space=pltpu.VMEM)
    hbm = pl.BlockSpec(memory_space=pl.ANY)
    return pl.pallas_call(
        main_body,
        out_shape=(
            jax.ShapeDtypeStruct((SIDE, SIDE), F32),
            jax.ShapeDtypeStruct((wide, BLOCK), BF16),
            jax.ShapeDtypeStruct((1, SIDE), F32),
        ),
        in_specs=[vmem, vmem, hbm],
        out_specs=(vmem, hbm, vmem),
        scratch_shapes=[
            pltpu.VMEM((wide, BLOCK), BF16),
            pltpu.VMEM((wide, BLOCK), BF16),
            pltpu.VMEM((BLOCK, BLOCK), BF16),
            pltpu.VMEM((BLOCK, 1), F32),
            pltpu.VMEM((1, BLOCK), F32),
            pltpu.VMEM((BLOCK, 2 * SIDE), BF16),
            pltpu.VMEM((BLOCK, 2 * SIDE), F32),
            pltpu.VMEM((BLOCK, 2 * SIDE), BF16),
            pltpu.VMEM((BLOCK, SIDE), F32),
            pltpu.VMEM((BLOCK, SIDE), BF16),
            pltpu.SemaphoreType.DMA((1,)),
            pltpu.SemaphoreType.DMA((BLOCK // TILE,)),
        ],
        compiler_params=pltpu.CompilerParams(vmem_limit_bytes=56 * 1024 * 1024),
    )(
        pltpu.with_memory_space_constraint(own, pltpu.VMEM),
        pltpu.with_memory_space_constraint(twin, pltpu.VMEM),
        gradient,
    )


def shifted(x, axis, step):
    size = lax.axis_size(axis)
    return lax.ppermute(x, axis, [(i, (i + step) % size) for i in range(size)])


def gathered(half):
    up, down = shifted(half, "row", 1), shifted(half, "row", -1)
    up2, down2 = shifted(half, "row", 2), shifted(half, "row", -2)
    near = jnp.stack([half, up, down, up2, down2])
    near_over, near_under = shifted(near, "col", 2), shifted(near, "col", -2)
    up3, down3 = shifted(up, "row", 2), shifted(down, "row", -2)
    up4 = shifted(up2, "row", 2)
    rest = jnp.stack([up3, down3, up4])
    rest_over, rest_under = shifted(rest, "col", 2), shifted(rest, "col", -2)
    far = [shifted(near_over, "col", 2), shifted(rest_under, "col", -2)]
    early = jnp.concatenate([near, rest, near_over, near_under])
    late = jnp.concatenate([rest_over, rest_under, *far])
    return early, late


def local(statistic, gradient):
    early, late = gathered(prep(statistic))
    twins = []
    for part in (early, late):
        twins.append(lax.ppermute(part, "col", [(i, i ^ 1) for i in range(GRID)]))
    own, twin = jnp.concatenate([early, late]), jnp.concatenate(twins)
    next_m, preconditioned, next_diag = main(own, twin, gradient.T)
    return (next_m, preconditioned.T, next_diag.reshape(SIDE))


def solution(mesh):
    return jax.shard_map(
        local,
        mesh=mesh,
        in_specs=(P(("section", "row"), "col"), P("section", ("row", "col"))),
        out_specs=(
            P(("section", "row"), "col"),
            P("section", ("row", "col")),
            P(("section", "row")),
        ),
        check_vma=False,
    )
```

```python
import jax
import jax.numpy as jnp
from jax import lax
from jax.experimental import pallas as pl
from jax.experimental.pallas import tpu as pltpu
from jax.sharding import PartitionSpec as P

BLOCK = 2048
SIDE = 256
HALF = 128
ROWS = 144
GRID = 8
F32 = jnp.float32
BF16 = jnp.bfloat16


def eye_mask(n):
    a = lax.broadcasted_iota(jnp.int32, (n, n), 0)
    b = lax.broadcasted_iota(jnp.int32, (n, n), 1)
    return a, b


def three_parts(x):
    hi = x.astype(BF16)
    rest = x - hi.astype(F32)
    mid = rest.astype(BF16)
    low = (rest - mid.astype(F32)).astype(BF16)
    return [hi.astype(F32), mid.astype(F32), low.astype(F32)]


def prep_body(s_ref, out_ref):
    row, col = lax.axis_index("row"), lax.axis_index("col")
    s = s_ref[...]
    a, b = eye_mask(SIDE)
    squares = jnp.sum(s * s, axis=0, keepdims=True)
    diag = jnp.sum(jnp.where((a == b) & (row == col), s, 0.0), axis=0, keepdims=True)
    tail = three_parts(diag) + three_parts(squares) + [jnp.zeros((ROWS - HALF - 6, SIDE), F32)]
    out_ref[HALF:, :] = jnp.concatenate(tail, axis=0).astype(BF16)

    @pl.when(row < col)
    def _():
        out_ref[:HALF, :] = s[:HALF, :].astype(BF16)

    @pl.when(row > col)
    def _():
        out_ref[:HALF, :] = s[:, HALF:].T.astype(BF16)

    @pl.when(row == col)
    def _():
        p, q = eye_mask(HALF)
        upper = jnp.where(p < q, s[:HALF, :HALF], 0.0)
        lower = jnp.where(p > q, s[HALF:, HALF:], 0.0)
        out_ref[:HALF, :HALF] = (upper + lower).astype(BF16)
        out_ref[:HALF, HALF:] = s[:HALF, HALF:].astype(BF16)


def prep(statistic):
    return pl.pallas_call(
        prep_body,
        out_shape=jax.ShapeDtypeStruct((ROWS, SIDE), BF16),
        in_specs=[pl.BlockSpec(memory_space=pltpu.VMEM)],
        out_specs=pl.BlockSpec(memory_space=pltpu.VMEM),
    )(statistic)


def block_of(size, index):
    return pl.ds(pl.multiple_of(index * size, size), size)


TILE = 1024


def main_body(own_ref, twin_ref, g_hbm, m_ref, pre_hbm, nd_ref, g_ref, pre_ref,
              o_ref, dcol_ref, drow_ref, v_ref, t_ref, th_ref, third_ref, ob_ref,
              in_sem, out_sem):
    row, col = lax.axis_index("row"), lax.axis_index("col")
    core = lax.rem(col, 2)
    a, b = eye_mask(SIDE)
    same = a == b
    p, q = eye_mask(HALF)
    arrival = pltpu.make_async_copy(g_hbm, g_ref, in_sem.at[0])
    arrival.start()

    def ring_slot(offset, size):
        middle = size // 2
        return jnp.where(
            offset < middle, 2 * offset, jnp.where(offset == middle, size - 1, 2 * (size - offset) - 1)
        )

    row_slot = [ring_slot(lax.rem(i - row + GRID, GRID), GRID) for i in range(GRID)]
    pair = col // 2
    pair_slot = [ring_slot(lax.rem(j - pair + 4, 4), 4) for j in range(4)]

    def slot_of(j, line):
        over, under, far = pair_slot[j] == 1, pair_slot[j] == 2, pair_slot[j] == 3
        first = jnp.where(over, 8, jnp.where(under, 13, jnp.where(far, 24, 0)))
        then = jnp.where(over, 13, jnp.where(under, 16, jnp.where(far, 24, 0)))
        return line + jnp.where(line < 5, first, then)

    def above(half, i, there):
        o_ref[i * SIDE : i * SIDE + HALF, there] = half
        o_ref[there, i * SIDE : i * SIDE + HALF] = half.T

    def below(half, second, i):
        o_ref[second, i * SIDE : (i + 1) * SIDE] = half
        o_ref[i * SIDE : (i + 1) * SIDE, second] = half.T

    def middle(half, i):
        first = slice(i * SIDE, i * SIDE + HALF)
        second = slice(i * SIDE + HALF, (i + 1) * SIDE)
        mixed = half[:, :HALF].astype(F32)
        corner = half[:, HALF:]
        upper = jnp.where(p < q, mixed, 0.0)
        lower = jnp.where(p > q, mixed, 0.0)
        o_ref[first, first] = (upper + upper.T).astype(BF16)
        o_ref[second, second] = (lower + lower.T).astype(BF16)
        o_ref[first, second] = corner
        o_ref[second, first] = corner.T

    def assemble(pieces_ref, parity):
        total = jnp.zeros((1, SIDE), F32)
        for j in range(4):
            there = block_of(SIDE, 2 * j + parity)
            second = pl.ds(pl.multiple_of((2 * j + parity) * SIDE + HALF, HALF), HALF)
            for i in range(GRID):
                slot = slot_of(j, row_slot[i])
                tail = pieces_ref[slot, HALF:ROWS, :].astype(F32)
                total = total + (tail[3:4] + tail[4:5] + tail[5:6])
                if i == 2 * j:

                    @pl.when(parity == 0)
                    def _():
                        middle(pieces_ref[slot, :HALF, :], i)

                    @pl.when(parity == 1)
                    def _():
                        above(pieces_ref[slot, :HALF, :], i, there)

                elif i == 2 * j + 1:

                    @pl.when(parity == 1)
                    def _():
                        middle(pieces_ref[slot, :HALF, :], i)

                    @pl.when(parity == 0)
                    def _():
                        below(pieces_ref[slot, :HALF, :], second, i)

                elif i < 2 * j:
                    above(pieces_ref[slot, :HALF, :], i, there)
                else:
                    below(pieces_ref[slot, :HALF, :], second, i)
            slot = slot_of(j, jnp.where(parity == 0, row_slot[2 * j], row_slot[2 * j + 1]))
            tail = pieces_ref[slot, HALF:ROWS, :].astype(F32)
            drow = tail[0:1] + tail[1:2] + tail[2:3]
            drow_ref[:, there] = drow
            dcol_ref[there, :] = jnp.sum(jnp.where(same, drow, 0.0), axis=1, keepdims=True)
        return total

    squares = assemble(own_ref, core) + assemble(twin_ref, 1 - core)
    ss = jnp.full((1, 1), jnp.sum(squares), F32)
    scale = jnp.sqrt(BLOCK * (ss / (BLOCK * BLOCK) + 1e-06))
    inv = 1.0 / scale
    root = lax.rsqrt(jnp.sqrt(scale))

    arrival.wait()

    def leave(n):
        cols = block_of(TILE, n)
        return pltpu.make_async_copy(pre_ref.at[:, cols], pre_hbm.at[:, cols], out_sem.at[n])

    far_by = 0.25 * inv * root

    def spread(n, _):
        cols = block_of(TILE, n)
        w = jnp.dot(g_ref[...], o_ref[:, cols], preferred_element_type=F32)
        near_by = (1.25 * root) - far_by * drow_ref[:, cols]
        pre_ref[:, cols] = (near_by * g_ref[:, cols].astype(F32) - far_by * w).astype(BF16)
        leave(n).start()
        return 0

    lax.fori_loop(0, BLOCK // TILE, spread, 0, unroll=True)

    v_ref[:, :SIDE] = o_ref[:, block_of(SIDE, row)]
    v_ref[:, SIDE:] = o_ref[:, block_of(SIDE, col)]
    d_cols = jnp.concatenate([drow_ref[:, block_of(SIDE, row)], drow_ref[:, block_of(SIDE, col)]], axis=1)
    second_by = 0.0625 * inv * inv
    by_col = second_by * d_cols - 0.625 * inv

    def two(n, _):
        rows = block_of(TILE, n)
        w = jnp.dot(o_ref[rows, :], v_ref[...], preferred_element_type=F32)
        t = (second_by * dcol_ref[rows, :] + by_col) * v_ref[rows, :].astype(F32) + second_by * w
        t_ref[rows, :] = t
        th_ref[rows, :] = t.astype(BF16)
        return 0

    lax.fori_loop(0, BLOCK // TILE, two, 0, unroll=True)

    ones = d_cols * inv
    alone = (25.0 - 10.0 * ones + ones * ones) * 0.0625
    diags = []
    for place, lanes in ((row, slice(0, SIDE)), (col, slice(SIDE, 2 * SIDE))):
        rows = block_of(SIDE, place)
        t = t_ref[rows, lanes] + jnp.where(same, alone[:, lanes], 0.0)
        t_ref[rows, lanes] = t
        th_ref[rows, lanes] = jnp.where(same, 0.0, t).astype(BF16)
        diags.append(jnp.where(same, t, 0.0))
    e_cols = jnp.concatenate([jnp.sum(x, axis=0, keepdims=True) for x in diags], axis=1)
    e_row = jnp.sum(diags[0], axis=1, keepdims=True)
    e_by = e_cols * inv

    def three(n, acc):
        rows = block_of(TILE, n)
        w = jnp.dot(o_ref[rows, :], th_ref[...], preferred_element_type=F32)
        t = t_ref[rows, :]
        third = (dcol_ref[rows, :] * inv) * t + v_ref[rows, :].astype(F32) * e_by + w * inv
        third_ref[rows, :] = third[:, SIDE:]
        ob_ref[rows, :] = third[:, SIDE:].astype(BF16)
        return acc + jnp.sum(t[:, :SIDE] * third[:, :SIDE], axis=0, keepdims=True)

    nd_ref[...] = lax.fori_loop(0, BLOCK // TILE, three, jnp.zeros((1, SIDE), F32), unroll=True)

    rows = block_of(SIDE, col)
    third = third_ref[rows, :]
    ob_ref[rows, :] = jnp.where(same, 0.0, third).astype(BF16)
    third_col = jnp.sum(jnp.where(same, third, 0.0), axis=0, keepdims=True)
    inner = lax.dot_general(
        th_ref[:, :SIDE], ob_ref[...], (((0,), (0,)), ((), ())), preferred_element_type=F32
    )
    rows = block_of(SIDE, row)
    full = e_row * third_ref[rows, :] + t_ref[rows, SIDE:] * third_col + inner
    m_ref[...] = jnp.where(same & (row == col), 0.0, full)
    for n in range(BLOCK // TILE):
        leave(n).wait()


def main(own, twin, gradient):
    wide = gradient.shape[0]
    vmem = pl.BlockSpec(memory_space=pltpu.VMEM)
    hbm = pl.BlockSpec(memory_space=pl.ANY)
    return pl.pallas_call(
        main_body,
        out_shape=(
            jax.ShapeDtypeStruct((SIDE, SIDE), F32),
            jax.ShapeDtypeStruct((wide, BLOCK), BF16),
            jax.ShapeDtypeStruct((1, SIDE), F32),
        ),
        in_specs=[vmem, vmem, hbm],
        out_specs=(vmem, hbm, vmem),
        scratch_shapes=[
            pltpu.VMEM((wide, BLOCK), BF16),
            pltpu.VMEM((wide, BLOCK), BF16),
            pltpu.VMEM((BLOCK, BLOCK), BF16),
            pltpu.VMEM((BLOCK, 1), F32),
            pltpu.VMEM((1, BLOCK), F32),
            pltpu.VMEM((BLOCK, 2 * SIDE), BF16),
            pltpu.VMEM((BLOCK, 2 * SIDE), F32),
            pltpu.VMEM((BLOCK, 2 * SIDE), BF16),
            pltpu.VMEM((BLOCK, SIDE), F32),
            pltpu.VMEM((BLOCK, SIDE), BF16),
            pltpu.SemaphoreType.DMA((1,)),
            pltpu.SemaphoreType.DMA((BLOCK // TILE,)),
        ],
        compiler_params=pltpu.CompilerParams(vmem_limit_bytes=56 * 1024 * 1024),
    )(
        pltpu.with_memory_space_constraint(own, pltpu.VMEM),
        pltpu.with_memory_space_constraint(twin, pltpu.VMEM),
        gradient,
    )


def shifted(x, axis, step):
    size = lax.axis_size(axis)
    return lax.ppermute(x, axis, [(i, (i + step) % size) for i in range(size)])


def gathered(half):
    up, down = shifted(half, "row", 1), shifted(half, "row", -1)
    up2, down2 = shifted(half, "row", 2), shifted(half, "row", -2)
    near = jnp.stack([half, up, down, up2, down2])
    near_over, near_under = shifted(near, "col", 2), shifted(near, "col", -2)
    up3, down3 = shifted(up, "row", 2), shifted(down, "row", -2)
    up4 = shifted(up2, "row", 2)
    rest = jnp.stack([up3, down3, up4])
    rest_over, rest_under = shifted(rest, "col", 2), shifted(rest, "col", -2)
    back = jnp.concatenate([near_under[4:], rest_under])
    far = [shifted(near_over[:4], "col", 2), shifted(back, "col", -2)]
    early = jnp.concatenate([near, rest, near_over, near_under])
    late = jnp.concatenate([rest_over, rest_under, *far])
    return early, late


def local(statistic, gradient):
    early, late = gathered(prep(statistic))
    twins = []
    for part in (early, late):
        twins.append(lax.ppermute(part, "col", [(i, i ^ 1) for i in range(GRID)]))
    own, twin = jnp.concatenate([early, late]), jnp.concatenate(twins)
    next_m, preconditioned, next_diag = main(own, twin, gradient.T)
    return (next_m, preconditioned.T, next_diag.reshape(SIDE))


def solution(mesh):
    return jax.shard_map(
        local,
        mesh=mesh,
        in_specs=(P(("section", "row"), "col"), P("section", ("row", "col"))),
        out_specs=(
            P(("section", "row"), "col"),
            P("section", ("row", "col")),
            P(("section", "row")),
        ),
        check_vma=False,
    )
```
